32 devices in a mesh: groups: 2 (over x), ctx: 16 (over z, y, core).
Axes of the slice: x: 2, y: 2, z: 4, core: 2. Of those that a mesh axis runs over, the one named last changes fastest.
Arguments:
- features: bfloat16 [32768, 1024], P(('groups', 'ctx')), parts along dimension 0, may hold values from -6 to 6
- write_map: bfloat16 [32768, 128], P(('groups', 'ctx')), parts along dimension 0, may hold values from -6 to 6
- read_map: bfloat16 [32768, 128], P(('groups', 'ctx')), parts along dimension 0, may hold values from -3 to 3
- step_raw: float32 [32768, 16], P(('groups', 'ctx')), parts along dimension 0, may hold values from -3 to 3
- tokens: int32 [32768], P(('groups', 'ctx')), parts along dimension 0, may hold values from 0 to 4
- base_shift: float32 [5, 16], replicated, may hold values from -8 to -2
- decay_rate: float32 [16], replicated, may hold values from 0 to 2, as said below
- skip_gain: float32 [16], replicated, may hold values from 0.5 to 1.5
- cotangent: bfloat16 [32768, 1024], P(('groups', 'ctx')), parts along dimension 0, may hold values from -20 to 20
Outputs:
- layer_out: bfloat16 [32768, 1024], P(('groups', 'ctx')), parts along dimension 0
- grad_feature: bfloat16 [32768, 1024], P(('groups', 'ctx')), parts along dimension 0
- grad_write: bfloat16 [32768, 128], P(('groups', 'ctx')), parts along dimension 0
- grad_read: bfloat16 [32768, 128], P(('groups', 'ctx')), parts along dimension 0
- grad_step: float32 [32768, 16], P(('groups', 'ctx')), parts along dimension 0
- grad_skip: float32 [32], P('groups'), parts along dimension 0
The draws below stay inside these ranges and needn't reach their ends.
There are 2 independent parts, one for each index of `groups`. The reference program is written for one: setup_inputs(seed, part) draws one part's arguments, and reference() takes and returns one part's arrays. A program takes and returns all parts, laid end to end along the dimension named above; an argument that names none is the same for every part. Nothing has to cross between parts.
Inputs may be any that keep to these rules, and one draw needn't show every extreme that they name: `tokens`: 0, 1, 2, 3 stand for the bases A, C, G, T and 4 for an unknown base N. `decay_rate`: positive.
All inputs are finite; a program needn't handle non-finite values.
Results may differ from the reference program's by a relative error of at most 0.0015.
Values sent between devices are 32-bit elements; how exact they have to be, the bound alone decides.
A program may use at most 704 MiB of HBM per device.

```python
import math
import jax
import jax.numpy as jnp
from jax import lax

HEADS = 16
HEAD_DIM = 64
STATE_DIM = 128
SPAN = 256
ROWS = 1024
LENGTH = 16384


def head_kinds(key):
    key_count, key_order, key_slow, key_fast = jax.random.split(jax.random.fold_in(key, 11), 4)
    slow_count = jax.random.randint(key_count, (), max(1, HEADS // 4), HEADS - max(1, HEADS // 4) + 1)
    order = jax.random.permutation(key_order, HEADS)
    slow_heads = jnp.zeros((HEADS,), jnp.bool_).at[order].set(jnp.arange(HEADS) < slow_count)
    return (slow_heads, key_slow, key_fast)


def draw_decay_rate(key, part):
    slow_heads, key_slow, key_fast = head_kinds(key)
    slow_rate = 2.0 * jnp.exp(jax.random.uniform(key_slow, (HEADS,), jnp.float32, math.log(0.4), math.log(1.2))) / math.sqrt(LENGTH)
    fast_rate = jnp.exp(jax.random.uniform(key_fast, (HEADS,), jnp.float32, math.log(0.5), math.log(2.0)))
    return jnp.where(slow_heads, slow_rate, fast_rate).astype(jnp.float32)


def draw_base_shift(key, part):
    slow_heads, unused_slow, unused_fast = head_kinds(key)
    head_level = jnp.where(slow_heads, math.log(0.5 / math.sqrt(LENGTH)), math.log(0.03))
    jitter = jax.random.uniform(jax.random.fold_in(key, 23), (5, HEADS), jnp.float32, -0.5, 0.5)
    return (head_level[None, :] + jitter).astype(jnp.float32)


def draw_step_raw(key, part):
    key_noise, key_level = jax.random.split(jax.random.fold_in(key, 31))
    noise = jnp.clip(0.4 * jax.random.normal(key_noise, (LENGTH, HEADS), jnp.float32), -1.6, 1.6)
    offsets = jax.random.uniform(key_level, (LENGTH // ROWS, 1, HEADS), jnp.float32, -0.7, 0.7)
    spread_out = jnp.broadcast_to(offsets, (LENGTH // ROWS, ROWS, HEADS)).reshape(LENGTH, HEADS)
    return (noise + spread_out).astype(jnp.float32)


def draw_cotangent(key, part):
    rising = 1.0 + 2.0 * jnp.arange(LENGTH, dtype=jnp.float32) / (LENGTH - 1)
    raw_draw = jnp.clip(jax.random.normal(key, (LENGTH, HEADS * HEAD_DIM), jnp.float32), -4.0, 4.0)
    scaled = raw_draw * rising[:, None]
    return scaled.astype(jnp.bfloat16)


def touch_ends(values, key, least, high):
    dims = values.shape
    place = [jax.random.randint(jax.random.fold_in(key, axis), (), 0, dims[axis]) for axis in range(len(dims))]
    values = values.at[tuple(place)].set(least)
    longest = dims.index(max(dims))
    place[longest] = (place[longest] + 1) % dims[longest]
    return values.at[tuple(place)].set(high)


def steps_of(own_key, dims, cuts, low, largest):
    level, own = 1.0, jax.random.fold_in(own_key, 6)
    for position, parts in cuts:
        draws = jnp.exp(jax.random.uniform(jax.random.fold_in(own, position), (parts,), jnp.float32, low / len(cuts), largest / len(cuts)))
        level = level * jnp.repeat(draws, dims[position] // parts).reshape([-1 if axis == position else 1 for axis in range(len(dims))])
    return level


def scatter_about(rng, extent, scale, reach, cuts=(), kind=jnp.bfloat16):
    gain = steps_of(rng, extent, cuts, -0.22, 0.18) if cuts else 1.0
    values = jax.random.normal(rng, extent, jnp.float32) * scale * gain
    return jnp.minimum(jnp.maximum(values, -reach), reach).astype(kind)


def setup_inputs(seed: int = 0, part: int = 0) -> dict:
    keys = jax.random.split(jax.random.key(seed), 10)
    own_keys = jax.random.split(jax.random.fold_in(keys[9], part), 10)
    features = scatter_about(own_keys[0], (LENGTH, HEADS * HEAD_DIM), 1.0, 6.0, ((0, 16),))
    write_map = scatter_about(own_keys[1], (LENGTH, STATE_DIM), 1.0, 6.0, ((0, 16),))
    read_map = scatter_about(own_keys[2], (LENGTH, STATE_DIM), 0.5, 3.0, ((0, 16),))
    step_raw = draw_step_raw(jax.random.fold_in(jax.random.fold_in(keys[9], part), 71), part)
    tokens = touch_ends(jax.random.randint(own_keys[4], (LENGTH,), 0, 5), jax.random.fold_in(own_keys[4], 1), 0, 4).astype(jnp.int32)
    base_shift = draw_base_shift(jax.random.fold_in(keys[9], 71), part)
    decay_rate = draw_decay_rate(jax.random.fold_in(keys[9], 71), part)
    skip_gain = jnp.clip(jax.random.uniform(keys[7], (HEADS,), jnp.float32, 0.5, 1.5), 0.5, 1.5)
    cotangent = draw_cotangent(jax.random.fold_in(jax.random.fold_in(keys[9], part), 71), part)
    return dict(features=features, write_map=write_map, read_map=read_map, step_raw=step_raw, tokens=tokens, base_shift=base_shift, decay_rate=decay_rate, skip_gain=skip_gain, cotangent=cotangent)


PRECISE = lax.Precision.HIGHEST
MASKED = 10000.0

def step_rates(step_raw, base_shift, tokens):
    base_codes = jnp.arange(5, dtype=jnp.int32)
    onehot = (tokens[:, None] == base_codes[None, :]).astype(jnp.float32)
    paired = jnp.where(tokens < 4, 3 - tokens, tokens).astype(jnp.int32)
    onehot_rc = (paired[:, None] == base_codes[None, :]).astype(jnp.float32)
    step_fwd = jax.nn.softplus(step_raw + jnp.dot(onehot, base_shift, precision=PRECISE))
    step_rc = jax.nn.softplus(step_raw + jnp.dot(onehot_rc, jnp.flip(base_shift, 1), precision=PRECISE))
    return (step_fwd, step_rc)

def block_step(memory, pieces, rate_vec):
    values, writes, reads, step_sizes = pieces
    block_len = values.shape[0]
    running = jnp.cumsum(step_sizes * rate_vec[None, :], axis=0)
    running_heads = running.T
    spread = running_heads[:, :, None] - running_heads[:, None, :]
    causal = jnp.tril(jnp.ones((block_len, block_len), dtype=jnp.bool_))
    fade_matrix = jnp.exp(-jnp.where(causal[None], spread, MASKED))
    scores = jnp.dot(reads, writes.T, precision=PRECISE)
    weights = fade_matrix * scores[None] * step_sizes.T[:, None, :]
    inner = jnp.einsum('hts,shp->thp', weights, values, precision=PRECISE)
    carried = jnp.exp(-running)[:, :, None] * jnp.einsum('tn,hpn->thp', reads, memory, precision=PRECISE)
    tail_weight = jnp.exp(running - running[-1][None, :]) * step_sizes
    updated = jnp.exp(-running[-1])[:, None, None] * memory + jnp.einsum('sh,shp,sn->hpn', tail_weight, values, writes, precision=PRECISE)
    return (updated, inner + carried)

def ssd_scan(values, writes, reads, step_sizes, rate_vec):
    block_count = LENGTH // SPAN

    def blocked(array):
        return array.reshape((block_count, SPAN) + array.shape[1:])

    def advance(memory, pieces):
        return block_step(memory, pieces, rate_vec)
    initial = jnp.zeros((HEADS, HEAD_DIM, STATE_DIM), jnp.float32)
    unused_final, emitted = lax.scan(jax.checkpoint(advance), initial, (blocked(values), blocked(writes), blocked(reads), blocked(step_sizes)))
    return emitted.reshape(LENGTH, HEADS, HEAD_DIM)

def mixed_layer(values, writes, reads, step_raw, skip_gain, base_shift, decay_rate, tokens):
    step_fwd, step_rc = step_rates(step_raw, base_shift, tokens)
    y_fwd = ssd_scan(values, writes, reads, step_fwd, decay_rate)
    y_rc = jnp.flip(ssd_scan(jnp.flip(values, 0), jnp.flip(writes, 0), jnp.flip(reads, 0), jnp.flip(step_rc, 0), jnp.flip(decay_rate)), 0)
    return y_fwd + y_rc + (skip_gain + jnp.flip(skip_gain))[None, :, None] * values

def reference(features, write_map, read_map, step_raw, tokens, base_shift, decay_rate, skip_gain, cotangent):
    values = features.astype(jnp.float32).reshape(LENGTH, HEADS, HEAD_DIM)
    writes = write_map.astype(jnp.float32)
    reads = read_map.astype(jnp.float32)

    def layer_fn(value_in, write_in, read_in, raw_in, gain_in):
        return mixed_layer(value_in, write_in, read_in, raw_in, gain_in, base_shift, decay_rate, tokens)
    mixed, pullback = jax.vjp(layer_fn, values, writes, reads, step_raw, skip_gain)
    grads = pullback(cotangent.astype(jnp.float32).reshape(LENGTH, HEADS, HEAD_DIM))
    norm_scale = 1.0 / math.sqrt(LENGTH * HEAD_DIM)
    return (mixed.reshape(LENGTH, HEADS * HEAD_DIM).astype(jnp.bfloat16), grads[0].reshape(LENGTH, HEADS * HEAD_DIM).astype(jnp.bfloat16), grads[1].astype(jnp.bfloat16), grads[2].astype(jnp.bfloat16), grads[3], grads[4] * norm_scale)
```

```python
import math

import jax
import jax.numpy as jnp
from jax import lax
from jax.sharding import PartitionSpec as P

SPAN = 128
EXACT = lax.Precision.HIGHEST
HIGH = lax.Precision.HIGH
F32 = jnp.float32


def ein(spec, a, b, precision=HIGH):
    return jnp.einsum(spec, a, b, precision=precision, preferred_element_type=F32)


def scan_over_devices(zone, lams, count, place, reverse):
    sign = -1 if reverse else 1

    def shifted(array, step):
        pairs = [(i, i + sign * step) for i in range(count) if 0 <= i + sign * step < count]
        return lax.ppermute(array, "ctx", pairs)

    state = shifted(zone, 1)
    if count <= 2:
        return state
    logs = lams
    window = 1
    while window < count - 1:
        ids = jnp.arange(count)
        if reverse:
            inside = (ids > place) & (ids <= place + window)
        else:
            inside = (ids < place) & (ids >= place - window)
        weight = jnp.exp(-jnp.sum(jnp.where(inside[:, None, None], logs, 0.0), axis=0))
        state = state + weight[:, :, None] * shifted(state, window)
        window *= 2
    return state


def per_device(
    features, write_map, read_map, step_raw, tokens, base_shift, decay_rate, skip_gain, cotangent
):
    rows, width = features.shape
    heads = decay_rate.shape[0]
    size = width // heads
    span = min(SPAN, rows)
    blocks = rows // span
    count = lax.axis_size("ctx")
    place = lax.axis_index("ctx")
    rates = jnp.concatenate([decay_rate, jnp.flip(decay_rate)])

    codes = jnp.arange(5, dtype=jnp.int32)
    onehot = (tokens[:, None] == codes[None, :]).astype(F32)
    table = jnp.concatenate([base_shift, jnp.flip(base_shift[jnp.array([3, 2, 1, 0, 4])], 1)], 1)
    logits = jnp.concatenate([step_raw, step_raw], 1) + jnp.dot(onehot, table, precision=EXACT)
    steps = jax.nn.softplus(logits)
    slopes = jax.nn.sigmoid(logits)

    fsteps, rsteps = steps[:, :heads], steps[:, heads:]
    drops = (steps * rates[None, :]).reshape(blocks, span, 2 * heads)
    lower = jnp.tril(jnp.ones((span, span), F32))
    upper = lower.T
    strict_lower = lower - jnp.eye(span, dtype=F32)
    strict_upper = strict_lower.T

    def along(tri, array):
        return ein("ts,ksh->kth", tri, array, EXACT)

    rf = along(lower, drops[..., :heads])
    rr = along(upper, drops[..., heads:])
    tot_f, tot_r = rf[:, -1], rr[:, 0]
    ef, er = jnp.exp(-rf), jnp.exp(-rr)
    tf = jnp.exp(rf - tot_f[:, None])
    tr = jnp.exp(rr - tot_r[:, None])
    sf = fsteps.reshape(blocks, span, heads)
    sr = rsteps.reshape(blocks, span, heads)

    expand = (jnp.arange(heads)[:, None] == jnp.arange(width)[None, :] // size).astype(F32)

    def wide(array):
        return jnp.einsum("kth,hw->ktw", array, expand, precision=EXACT)

    def narrow(array):
        return jnp.einsum("ktw,hw->kth", array, expand, precision=HIGH)

    xb = features.reshape(blocks, span, width)
    yb = cotangent.reshape(blocks, span, width)
    bb = write_map.reshape(blocks, span, -1)
    cb = read_map.reshape(blocks, span, -1)
    x32, y32 = xb.astype(F32), yb.astype(F32)
    b32, c32 = bb.astype(F32), cb.astype(F32)

    ef_w, er_w = wide(ef), wide(er)
    xf, xr = wide(tf * sf) * x32, wide(tr * sr) * x32
    yf, yr = ef_w * y32, er_w * y32
    bs_f = ein("ksw,ksn->kwn", xf, b32)
    bs_r = ein("ksw,ksn->kwn", xr, b32)
    ab_f = ein("ktw,ktn->kwn", yf, c32)
    ab_r = ein("ktw,ktn->kwn", yr, c32)

    def columns(array):
        return jnp.repeat(array, size, axis=-1)

    fade_f, fade_r = columns(jnp.exp(-tot_f)), columns(jnp.exp(-tot_r))

    def block_scan(fades, parts, reverse):
        order = range(blocks - 1, -1, -1) if reverse else range(blocks)
        state, weight = jnp.zeros_like(parts[0]), jnp.ones_like(fades[0])
        states, weights = [None] * blocks, [None] * blocks
        for k in order:
            states[k], weights[k] = state, weight
            state = fades[k][:, None] * state + parts[k]
            weight = weight * fades[k]
        return states, weights, state

    sf_loc, sf_wt, zone_f = block_scan(fade_f, bs_f, False)
    sr_loc, sr_wt, zone_r = block_scan(fade_r, bs_r, True)
    af_loc, af_wt, back_f = block_scan(fade_f, ab_f, True)
    ar_loc, ar_wt, back_r = block_scan(fade_r, ab_r, False)

    logs = lax.all_gather(jnp.stack([jnp.sum(tot_f, 0), jnp.sum(tot_r, 0)]), "ctx")
    logs = columns(logs)
    ahead = scan_over_devices(jnp.stack([zone_f, back_r]), logs, count, place, False)
    behind = scan_over_devices(jnp.stack([back_f, zone_r]), logs, count, place, True)

    def entered(local, weights, entry):
        return jnp.stack([s + w[:, None] * entry for s, w in zip(local, weights)])

    state_f = entered(sf_loc, sf_wt, ahead[0])
    state_r = entered(sr_loc, sr_wt, behind[1])
    adj_f = entered(af_loc, af_wt, behind[0])
    adj_r = entered(ar_loc, ar_wt, ahead[1])

    def heads_first(array):
        return jnp.transpose(array.reshape(blocks, span, heads, size), (2, 0, 1, 3))

    xh, yh = heads_first(xb), heads_first(yb)
    turned = lambda array: jnp.transpose(array, (2, 0, 1))
    rf_h, rr_h, sf_h, sr_h = turned(rf), turned(rr), turned(sf), turned(sr)
    t_pos = lax.broadcasted_iota(jnp.int32, (span, span), 0)[None, None]
    s_pos = lax.broadcasted_iota(jnp.int32, (span, span), 1)[None, None]
    spread = jnp.where(
        t_pos >= s_pos,
        rf_h[..., :, None] - rf_h[..., None, :],
        rr_h[..., :, None] - rr_h[..., None, :],
    )
    fade = jnp.exp(-spread)
    size_s = jnp.where(
        t_pos > s_pos,
        sf_h[..., None, :],
        jnp.where(t_pos < s_pos, sr_h[..., None, :], (sf_h + sr_h)[..., None, :]),
    )
    mask = fade * size_s
    scores = ein("ktn,ksn->kts", cb, bb, None)
    weights = mask * scores[None]
    crossed = ein("hktp,hksp->hkts", yh, xh, None)
    d_scores = jnp.sum(crossed * mask, axis=0)
    inner_y = ein("hkts,hksp->hktp", weights, xh.astype(F32))
    inner_x = ein("hkts,hktp->hksp", weights, yh.astype(F32))
    quota = crossed * scores[None] * fade
    pull = quota * size_s
    low, high = t_pos > s_pos, t_pos < s_pos
    back = lambda array: jnp.transpose(array, (1, 2, 0))
    qf = back(jnp.sum(jnp.where(low, quota, 0.0), axis=2))
    qr = back(jnp.sum(jnp.where(high, quota, 0.0), axis=2))
    zf = back(jnp.sum(jnp.where(low, pull, 0.0), axis=3))
    zr = back(jnp.sum(jnp.where(high, pull, 0.0), axis=3))
    flat = lambda array: jnp.transpose(array, (1, 2, 0, 3)).reshape(blocks, span, width)

    both = narrow(x32 * y32)
    center = jnp.sum(c32 * b32, axis=-1)[..., None] * both

    v_f = ein("ktn,kwn->ktw", c32, state_f)
    v_r = ein("ktn,kwn->ktw", c32, state_r)
    u_f = ein("ksn,kwn->ksw", b32, adj_f)
    u_r = ein("ksn,kwn->ksw", b32, adj_r)
    gain = columns(skip_gain + jnp.flip(skip_gain))
    mixed = flat(inner_y) + ef_w * v_f + er_w * v_r + gain * x32
    grad_x = flat(inner_x) + wide(tf * sf) * u_f + wide(tr * sr) * u_r + gain * y32
    grad_c = (
        ein("kts,ksn->ktn", d_scores, b32)
        + ein("ktw,kwn->ktn", yf, state_f)
        + ein("ktw,kwn->ktn", yr, state_r)
    )
    grad_b = (
        ein("kts,ktn->ksn", d_scores, c32)
        + ein("ksw,kwn->ksn", xf, adj_f)
        + ein("ksw,kwn->ksn", xr, adj_r)
    )
    xu_f, xu_r = tf * narrow(x32 * u_f), tr * narrow(x32 * u_r)
    yv_f, yv_r = ef * narrow(y32 * v_f), er * narrow(y32 * v_r)

    def per_head(array):
        return jnp.sum(array.reshape(blocks, heads, -1), axis=-1)

    hold_f = jnp.exp(-tot_f) * per_head(state_f * adj_f)
    hold_r = jnp.exp(-tot_r) * per_head(state_r * adj_r)
    drop_f = (
        along(upper, sf * qf - zf - yv_f) - along(strict_lower, sf * xu_f) - hold_f[:, None]
    )
    drop_r = (
        along(lower, sr * qr - zr - yv_r) - along(strict_upper, sr * xu_r) - hold_r[:, None]
    )
    d_f = (qf + center + xu_f + rates[:heads] * drop_f).reshape(rows, heads)
    d_r = (qr + center + xu_r + rates[heads:] * drop_r).reshape(rows, heads)
    grad_s = d_f * slopes[:, :heads] + d_r * slopes[:, heads:]
    own_gain = jnp.sum(both, axis=(0, 1))
    gains = lax.psum(own_gain + jnp.flip(own_gain), "ctx")
    norm_scale = 1.0 / math.sqrt(rows * count * size)
    return (
        mixed.reshape(rows, width).astype(jnp.bfloat16),
        grad_x.reshape(rows, width).astype(jnp.bfloat16),
        grad_b.reshape(rows, -1).astype(jnp.bfloat16),
        grad_c.reshape(rows, -1).astype(jnp.bfloat16),
        grad_s,
        gains * norm_scale,
    )


def solution(mesh):
    split = P(("groups", "ctx"), None)
    return jax.shard_map(
        per_device,
        mesh=mesh,
        in_specs=(split, split, split, split, P(("groups", "ctx")), P(), P(), P(), split),
        out_specs=(split, split, split, split, split, P("groups")),
        check_vma=False,
    )
```

```python
import math

import jax
import jax.numpy as jnp
from jax import lax
from jax.sharding import PartitionSpec as P

SPAN = 128
EXACT = lax.Precision.HIGHEST
HIGH = lax.Precision.HIGH
F32 = jnp.float32


def ein(spec, a, b, precision=HIGH):
    return jnp.einsum(spec, a, b, precision=precision, preferred_element_type=F32)


def scan_over_devices(zone, logs, count, size, reverse):
    sign = -1 if reverse else 1

    def shifted(array, step):
        pairs = [(i, i + sign * step) for i in range(count) if 0 <= i + sign * step < count]
        return lax.ppermute(array, "ctx", pairs)

    state, gone = shifted(zone, 1), shifted(logs, 1)
    window = 1
    while window < count - 1:
        weight = jnp.repeat(jnp.exp(-gone), size, axis=-1)
        state = state + weight[:, :, None] * shifted(state, window)
        gone = gone + shifted(gone, window)
        window *= 2
    return state


def sum_over_devices(array, count):
    if count & (count - 1):
        return lax.psum(array, "ctx")
    step = 1
    while step < count:
        array = array + lax.ppermute(array, "ctx", [(i, i ^ step) for i in range(count)])
        step *= 2
    return array


def per_device(
    features, write_map, read_map, step_raw, tokens, base_shift, decay_rate, skip_gain, cotangent
):
    rows, width = features.shape
    heads = decay_rate.shape[0]
    size = width // heads
    span = min(SPAN, rows)
    blocks = rows // span
    count = lax.axis_size("ctx")
    rates = jnp.concatenate([decay_rate, jnp.flip(decay_rate)])

    codes = jnp.arange(5, dtype=jnp.int32)
    onehot = (tokens[:, None] == codes[None, :]).astype(F32)
    table = jnp.concatenate([base_shift, jnp.flip(base_shift[jnp.array([3, 2, 1, 0, 4])], 1)], 1)
    logits = jnp.concatenate([step_raw, step_raw], 1) + jnp.dot(onehot, table, precision=EXACT)
    steps = jax.nn.softplus(logits)
    slopes = jax.nn.sigmoid(logits)

    fsteps, rsteps = steps[:, :heads], steps[:, heads:]
    drops = (steps * rates[None, :]).reshape(blocks, span, 2 * heads)
    lower = jnp.tril(jnp.ones((span, span), F32))
    upper = lower.T
    strict_lower = lower - jnp.eye(span, dtype=F32)
    strict_upper = strict_lower.T

    def along(tri, array):
        return ein("ts,ksh->kth", tri, array, EXACT)

    rf = along(lower, drops[..., :heads])
    rr = along(upper, drops[..., heads:])
    tot_f, tot_r = rf[:, -1], rr[:, 0]
    ef, er = jnp.exp(-rf), jnp.exp(-rr)
    tf = jnp.exp(rf - tot_f[:, None])
    tr = jnp.exp(rr - tot_r[:, None])
    sf = fsteps.reshape(blocks, span, heads)
    sr = rsteps.reshape(blocks, span, heads)

    expand = (jnp.arange(heads)[:, None] == jnp.arange(width)[None, :] // size).astype(F32)

    def wide(array):
        return jnp.einsum("kth,hw->ktw", array, expand, precision=HIGH)

    def narrow(array):
        return jnp.einsum("ktw,hw->kth", array, expand, precision=HIGH)

    xb = features.reshape(blocks, span, width)
    yb = cotangent.reshape(blocks, span, width)
    bb = write_map.reshape(blocks, span, -1)
    cb = read_map.reshape(blocks, span, -1)
    x32, y32 = xb.astype(F32), yb.astype(F32)
    b32, c32 = bb.astype(F32), cb.astype(F32)

    ef_w, er_w = wide(ef), wide(er)
    xf, xr = wide(tf * sf) * x32, wide(tr * sr) * x32
    yf, yr = ef_w * y32, er_w * y32
    bs_f = ein("ksw,ksn->kwn", xf, b32)
    bs_r = ein("ksw,ksn->kwn", xr, b32)
    ab_f = ein("ktw,ktn->kwn", yf, c32)
    ab_r = ein("ktw,ktn->kwn", yr, c32)

    def columns(array):
        return jnp.repeat(array, size, axis=-1)

    fade_f, fade_r = columns(jnp.exp(-tot_f)), columns(jnp.exp(-tot_r))

    def block_scan(fades, parts, reverse):
        order = range(blocks - 1, -1, -1) if reverse else range(blocks)
        state, weight = jnp.zeros_like(parts[0]), jnp.ones_like(fades[0])
        states, weights = [None] * blocks, [None] * blocks
        for k in order:
            states[k], weights[k] = state, weight
            state = fades[k][:, None] * state + parts[k]
            weight = weight * fades[k]
        return states, weights, state

    sf_loc, sf_wt, zone_f = block_scan(fade_f, bs_f, False)
    sr_loc, sr_wt, zone_r = block_scan(fade_r, bs_r, True)
    af_loc, af_wt, back_f = block_scan(fade_f, ab_f, True)
    ar_loc, ar_wt, back_r = block_scan(fade_r, ab_r, False)

    logs = jnp.stack([jnp.sum(tot_f, 0), jnp.sum(tot_r, 0)])
    ahead = scan_over_devices(jnp.stack([zone_f, back_r]), logs, count, size, False)
    behind = scan_over_devices(jnp.stack([back_f, zone_r]), logs, count, size, True)

    def entered(local, weights, entry):
        return jnp.stack([s + w[:, None] * entry for s, w in zip(local, weights)])

    state_f = entered(sf_loc, sf_wt, ahead[0])
    state_r = entered(sr_loc, sr_wt, behind[1])
    adj_f = entered(af_loc, af_wt, behind[0])
    adj_r = entered(ar_loc, ar_wt, ahead[1])

    def heads_first(array):
        return jnp.transpose(array.reshape(blocks, span, heads, size), (2, 0, 1, 3))

    xh, yh = heads_first(xb), heads_first(yb)
    turned = lambda array: jnp.transpose(array, (2, 0, 1))
    rf_h, rr_h, sf_h, sr_h = turned(rf), turned(rr), turned(sf), turned(sr)
    t_pos = lax.broadcasted_iota(jnp.int32, (span, span), 0)[None, None]
    s_pos = lax.broadcasted_iota(jnp.int32, (span, span), 1)[None, None]
    spread = jnp.where(
        t_pos >= s_pos,
        rf_h[..., :, None] - rf_h[..., None, :],
        rr_h[..., :, None] - rr_h[..., None, :],
    )
    fade = jnp.exp(-spread)
    size_s = jnp.where(
        t_pos > s_pos,
        sf_h[..., None, :],
        jnp.where(t_pos < s_pos, sr_h[..., None, :], (sf_h + sr_h)[..., None, :]),
    )
    mask = fade * size_s
    scores = ein("ktn,ksn->kts", cb, bb, None)
    weights = mask * scores[None]
    crossed = ein("hktp,hksp->hkts", yh, xh, None)
    d_scores = jnp.sum(crossed * mask, axis=0)
    inner_y = ein("hkts,hksp->hktp", weights, xh.astype(F32))
    inner_x = ein("hkts,hktp->hksp", weights, yh.astype(F32))
    quota = crossed * scores[None] * fade
    pull = quota * size_s
    low, high = t_pos > s_pos, t_pos < s_pos
    back = lambda array: jnp.transpose(array, (1, 2, 0))
    qf = back(jnp.sum(jnp.where(low, quota, 0.0), axis=2))
    qr = back(jnp.sum(jnp.where(high, quota, 0.0), axis=2))
    zf = back(jnp.sum(jnp.where(low, pull, 0.0), axis=3))
    zr = back(jnp.sum(jnp.where(high, pull, 0.0), axis=3))
    flat = lambda array: jnp.transpose(array, (1, 2, 0, 3)).reshape(blocks, span, width)

    both = narrow(x32 * y32)
    center = jnp.sum(c32 * b32, axis=-1)[..., None] * both

    v_f = ein("ktn,kwn->ktw", c32, state_f)
    v_r = ein("ktn,kwn->ktw", c32, state_r)
    u_f = ein("ksn,kwn->ksw", b32, adj_f)
    u_r = ein("ksn,kwn->ksw", b32, adj_r)
    gain = columns(skip_gain + jnp.flip(skip_gain))
    mixed = flat(inner_y) + ef_w * v_f + er_w * v_r + gain * x32
    grad_x = flat(inner_x) + wide(tf * sf) * u_f + wide(tr * sr) * u_r + gain * y32
    grad_c = (
        ein("kts,ksn->ktn", d_scores, b32)
        + ein("ktw,kwn->ktn", yf, state_f)
        + ein("ktw,kwn->ktn", yr, state_r)
    )
    grad_b = (
        ein("kts,ktn->ksn", d_scores, c32)
        + ein("ksw,kwn->ksn", xf, adj_f)
        + ein("ksw,kwn->ksn", xr, adj_r)
    )
    xu_f, xu_r = tf * narrow(x32 * u_f), tr * narrow(x32 * u_r)
    yv_f, yv_r = ef * narrow(y32 * v_f), er * narrow(y32 * v_r)

    def per_head(array):
        return jnp.sum(array.reshape(blocks, heads, -1), axis=-1)

    hold_f = jnp.exp(-tot_f) * per_head(state_f * adj_f)
    hold_r = jnp.exp(-tot_r) * per_head(state_r * adj_r)
    drop_f = (
        along(upper, sf * qf - zf - yv_f) - along(strict_lower, sf * xu_f) - hold_f[:, None]
    )
    drop_r = (
        along(lower, sr * qr - zr - yv_r) - along(strict_upper, sr * xu_r) - hold_r[:, None]
    )
    d_f = (qf + center + xu_f + rates[:heads] * drop_f).reshape(rows, heads)
    d_r = (qr + center + xu_r + rates[heads:] * drop_r).reshape(rows, heads)
    grad_s = d_f * slopes[:, :heads] + d_r * slopes[:, heads:]
    own_gain = jnp.sum(both, axis=(0, 1))
    gains = sum_over_devices(own_gain + jnp.flip(own_gain), count)
    norm_scale = 1.0 / math.sqrt(rows * count * size)
    return (
        mixed.reshape(rows, width).astype(jnp.bfloat16),
        grad_x.reshape(rows, width).astype(jnp.bfloat16),
        grad_b.reshape(rows, -1).astype(jnp.bfloat16),
        grad_c.reshape(rows, -1).astype(jnp.bfloat16),
        grad_s,
        gains * norm_scale,
    )


def solution(mesh):
    split = P(("groups", "ctx"), None)
    return jax.shard_map(
        per_device,
        mesh=mesh,
        in_specs=(split, split, split, split, P(("groups", "ctx")), P(), P(), P(), split),
        out_specs=(split, split, split, split, split, P("groups")),
        check_vma=False,
    )
```
